512 devices in a mesh: row: 16 (over z_hi, x, core), col: 32 (over y, z_lo).
Axes of the slice: x: 4, y: 8, z: 8 (z_hi: 2, z_lo: 4; z = z_hi * 4 + z_lo), core: 2. Of those that a mesh axis runs over, the one named last changes fastest.
Arguments:
- row_factors: float32 [32, 512, 256], P('col', 'row'), may hold values from -1.5 to 1.5
- row_accum: float32 [32, 512, 256], P('col', 'row'), may hold values from 0.01 to 0.1
- row_marginals: int32 [32, 512], P('col'), may hold values from 256 to 4095
- col_factors: float32 [16, 32, 512, 256], P('row', 'col'), may hold values from -1.5 to 1.5
- col_accum: float32 [16, 32, 512, 256], P('row', 'col'), may hold values from 0.01 to 0.1
- col_marginals: int32 [16, 32, 512], P('row', 'col'), may hold values from 256 to 4095
- counts: int32 [2, 32, 512, 16, 512], P(None, 'col', None, 'row'), may hold values from 0 to 63, as said below
- plan: int32 [2], replicated, may hold values from 1 to 31, as said below
Outputs:
- new_rows: float32 [32, 512, 256], P('col', 'row')
- new_row_accum: float32 [32, 512, 256], P('col', 'row')
- new_columns: float32 [16, 32, 512, 256], P('row', 'col')
- new_column_accum: float32 [16, 32, 512, 256], P('row', 'col')
The draws below stay inside these ranges and needn't reach their ends.
Inputs may be any that keep to these rules, and one draw needn't show every extreme that they name: `counts`: zero means an unobserved pair. `plan`: equal on all devices; the masks of the rounds are distinct, and one round's mask is 31.
All inputs are finite; a program needn't handle non-finite values.
Results may differ from the reference program's by a relative error of at most 0.0003.
Values sent between devices are 32-bit elements; how exact they have to be, the bound alone decides.
A program may use at most 64 MiB of HBM per device.

```python
import math
import jax
import jax.numpy as jnp
from jax import lax

D = 256
CB = 512
RB = 512
ROUNDS = 2
N_ROW = 16
N_COL = 32


def draw_counts(key, part):
    shape = (ROUNDS, N_COL, RB, N_ROW, CB)
    values = jax.random.randint(jax.random.fold_in(key, 11), shape, 1, 64)
    keep = jax.random.randint(jax.random.fold_in(key, 12), shape, 0, 5)
    return jnp.where(keep >= 2, values, 0).astype(jnp.int32)


def draw_plan(key, part):
    order = (jax.random.permutation(jax.random.fold_in(key, 21), N_COL - 1) + 1).astype(jnp.int32)
    places = jnp.arange(N_COL - 1, dtype=jnp.int32)
    where_top = jnp.sum(jnp.where(order == N_COL - 1, places, 0)).astype(jnp.int32)
    target = jax.random.randint(jax.random.fold_in(key, 22), (), 0, ROUNDS).astype(jnp.int32)
    moved = order[target]
    order = jnp.where(places == target, N_COL - 1, jnp.where(places == where_top, moved, order))
    return order[:ROUNDS].astype(jnp.int32)


def plant(entries, own_key, smallest, largest):
    index_at = [jax.random.randint(jax.random.fold_in(own_key, axis), (), 0, length) for axis, length in enumerate(entries.shape)]
    longest = entries.shape.index(max(entries.shape))
    neighbour = index_at[:longest] + [(index_at[longest] + 1) % entries.shape[longest]] + index_at[longest + 1:]
    return entries.at[tuple(index_at)].set(smallest).at[tuple(neighbour)].set(largest)


def block_scale(stream_key, extent, cuts, smallest, top_value):
    def one(position, shards_of):
        steps = jax.random.uniform(jax.random.fold_in(jax.random.fold_in(stream_key, 6), position), (shards_of,), jnp.float32, smallest / len(cuts), top_value / len(cuts))
        return jnp.repeat(jnp.exp(steps), extent[position] // shards_of).reshape((-1,) + (1,) * (len(extent) - position - 1))

    factor_of = one(*cuts[0])
    for cut in cuts[1:]:
        factor_of = factor_of * one(*cut)
    return factor_of


def bell_draw(rng, extent, width, reach, shards=(), kind=jnp.bfloat16):
    result = jax.random.normal(rng, extent, jnp.float32) * width
    if len(shards) > 0:
        result = block_scale(rng, extent, shards, -0.22, 0.18) * result
    return jnp.clip(result, min=-reach, max=reach).astype(kind)


def setup_inputs(seed: int = 0) -> dict:
    key_of = jax.random.split(jax.random.key(seed), 9)
    return {
        "row_factors": bell_draw(key_of[0], (N_COL, RB, D), 0.25, 1.5, ((0, 32), (1, 16)), jnp.float32),
        "row_accum": jnp.clip(jnp.exp(math.log(0.1) - 2.3025851 * jax.random.uniform(key_of[1], (N_COL, RB, D), jnp.float32) ** block_scale(key_of[1], (N_COL, RB, D), ((0, 32), (1, 16)), -0.2, 0.2)), 0.01, 0.1),
        "row_marginals": plant(jax.random.randint(key_of[2], (N_COL, RB), 256, 4096), jax.random.fold_in(key_of[2], 1), 256, 4095).astype(jnp.int32),
        "col_factors": bell_draw(key_of[3], (N_ROW, N_COL, CB, D), 0.25, 1.5, ((0, 16), (1, 32)), jnp.float32),
        "col_accum": jnp.clip(jnp.exp(math.log(0.1) - 2.3025851 * jax.random.uniform(key_of[4], (N_ROW, N_COL, CB, D), jnp.float32) ** block_scale(key_of[4], (N_ROW, N_COL, CB, D), ((0, 16), (1, 32)), -0.2, 0.2)), 0.01, 0.1),
        "col_marginals": plant(jax.random.randint(key_of[5], (N_ROW, N_COL, CB), 256, 4096), jax.random.fold_in(key_of[5], 1), 256, 4095).astype(jnp.int32),
        "counts": draw_counts(jax.random.fold_in(key_of[8], 71), 0),
        "plan": draw_plan(jax.random.fold_in(key_of[8], 71), 0),
    }


log_total = 11.5
learn_rate = 0.05

def tile_grad(counts_tile, pred, log_r, log_c, columns):
    target = jnp.log(jnp.maximum(counts_tile, 1).astype(jnp.float32)) + log_total - log_r - log_c
    confidence = 0.1 + 0.25 * jnp.sqrt(counts_tile.astype(jnp.float32))
    error = jnp.where(counts_tile > 0, confidence * (pred - target), jax.nn.sigmoid(pred - target))
    return error / columns

def reference(row_factors, row_accum, row_marginals, col_factors, col_accum, col_marginals, counts, plan):
    log_rows = jnp.log(row_marginals.astype(jnp.float32))
    held = jnp.swapaxes(col_factors, 0, 1)
    held_acc = jnp.swapaxes(col_accum, 0, 1)
    held_log = jnp.swapaxes(jnp.log(col_marginals.astype(jnp.float32)), 0, 1)
    highest = lax.Precision.HIGHEST
    for step in range(ROUNDS):
        source = jnp.bitwise_xor(jnp.arange(N_COL, dtype=jnp.int32), plan[step].astype(jnp.int32))
        held = held[source]
        held_acc = held_acc[source]
        held_log = held_log[source]
        tiles = counts[step]

        def one_block(items):
            w_rows, w_acc, l_rows, h_cols, h_acc, l_cols, tile = items
            pred = jnp.einsum('id,rkd->irk', w_rows, h_cols, precision=highest)
            error = tile_grad(tile, pred, l_rows[:, None, None], l_cols[None], CB)
            grad_w = jnp.einsum('irk,rkd->id', error, h_cols, precision=highest)
            grad_h = jnp.einsum('irk,id->rkd', error, w_rows, precision=highest)
            w_acc = w_acc + grad_w * grad_w
            w_rows = w_rows - learn_rate * grad_w / jnp.sqrt(w_acc)
            h_acc = h_acc + grad_h * grad_h
            h_cols = h_cols - learn_rate * grad_h / jnp.sqrt(h_acc)
            return (w_rows, w_acc, h_cols, h_acc)
        row_factors, row_accum, held, held_acc = lax.map(one_block, (row_factors, row_accum, log_rows, held, held_acc, held_log, tiles))
    return (row_factors, row_accum, jnp.swapaxes(held, 0, 1), jnp.swapaxes(held_acc, 0, 1))
```

```python
import functools

import jax
import jax.numpy as jnp
from jax import lax
from jax.experimental import pallas as pl
from jax.experimental.pallas import tpu as pltpu
from jax.sharding import PartitionSpec as P

log_total = 11.5
learn_rate = 0.05
MESH = pl.DeviceIdType.MESH

N_ROW, N_COL = 16, 32
RB, CB, D = 512, 512, 256
SH = RB // N_ROW
K = 4
KC = CB // K
RI = 256
f32, bf16 = jnp.float32, jnp.bfloat16


def flip(v, mask):
    out = v
    for b in range(5):
        if mask >> b & 1:
            out = out + (1 << b) * (1 - 2 * (v // (1 << b) % 2))
    return out


def split(a):
    hi = a.astype(bf16)
    return hi, (a - hi.astype(f32)).astype(bf16)


def dot3(a, b, dims):
    def d(p, q):
        return lax.dot_general(p, q, (dims, ((), ())), preferred_element_type=f32)

    return d(a[0], b[0]) + (d(a[0], b[1]) + d(a[1], b[0]))


def kernel(p0, p1, w_in, wa_in, lr_in, h_in, g_in, lc_in, cnt_in,
           w_out, wa_out, h_out, g_out,
           wf, whi, wlo, wa, lrt, hb, gb, lcb, cnt, gw, gh, r1, s1, r2, s2, r3, outh, outg,
           hs, hr, gs, gr, ls, lrs, ags, agr, s1s, s1r, s2s, s2r, s3s, s3r, loc, osem):
    r = lax.axis_index("row")
    c = lax.axis_index("col")
    zh, x, k = r // 8, r // 2 % 4, r % 2
    zp = (r + 8 - 16 * zh, c)
    cp = (r + 1 - 2 * k, c)
    xrow = [zh * 8 + (x + d) % 4 * 2 + k for d in (1, 2, 3)]
    xp = [(q, c) for q in xrow]
    c0, c1 = flip(c, p0), flip(c, p1)

    bar = pltpu.get_barrier_semaphore()
    for dev in [zp, cp, *xp, (r, c0), (r, c1)]:
        pl.semaphore_signal(bar, inc=1, device_id=dev, device_id_type=MESH)

    cl = [pltpu.make_async_copy(w_in, wf.at[0, pl.ds(r * SH, SH)], loc.at[0]),
          pltpu.make_async_copy(wa_in, wa, loc.at[1]),
          pltpu.make_async_copy(cnt_in.at[0], cnt.at[0], loc.at[2]),
          pltpu.make_async_copy(cnt_in.at[1], cnt.at[1], loc.at[3])]
    for q in cl:
        q.start()
    for i in range(4):
        lrt[pl.ds(i * 128, 128), :] = jnp.transpose(
            jnp.broadcast_to(lr_in[:, pl.ds(i * 128, 128)], (128, 128)))
    cl[0].wait()
    cl[1].wait()
    pl.semaphore_wait(bar, 7)

    def rows(q):
        return pl.ds(q * SH, SH)

    def agcopy(t, q, n, dev):
        ref = wf.at[t, rows(q)]
        return pltpu.make_async_remote_copy(ref, ref, ags.at[t, n], agr.at[t, q], device_id=dev, device_id_type=MESH)

    def own_sends(t):
        agcopy(t, r, 0, zp).start()
        for i in range(3):
            agcopy(t, r, 1 + i, xp[i]).start()
        agcopy(t, r, 4, cp).start()

    def gather(t):
        zq = r + 8 - 16 * zh
        agcopy(t, zq, 0, zp).wait_recv()
        for i in range(3):
            agcopy(t, zq, 5 + i, xp[i]).start()
        agcopy(t, zq, 8, cp).start()
        for i in range(3):
            agcopy(t, xrow[i], 0, cp).wait_recv()
            agcopy(t, xrow[i], 9 + i, cp).start()
        for i in range(3):
            q = xrow[i] + 8 - 16 * zh
            agcopy(t, q, 0, cp).wait_recv()
            agcopy(t, q, 12 + i, cp).start()
        for i in range(8):
            agcopy(t, i * 2 + 1 - k, 0, cp).wait_recv()
        for i in range(15):
            agcopy(t, r, i, cp).wait_send()

    def bulk(src, buf, ss, rs, t, j, dev):
        rr = pl.ds(j * KC, KC)
        return pltpu.make_async_remote_copy(src.at[rr], buf.at[t, rr], ss.at[t, j], rs.at[t, j], device_id=dev, device_id_type=MESH)

    def lcopy(src, t, dev):
        return pltpu.make_async_remote_copy(src, lcb.at[t], ls.at[t], lrs.at[t], device_id=dev, device_id_type=MESH)

    own_sends(0)
    lcopy(lc_in, 0, (r, c0)).start()
    for j in range(K):
        bulk(h_in, hb, hs, hr, 0, j, (r, c0)).start()
        bulk(g_in, gb, gs, gr, 0, j, (r, c0)).start()

    def out_copies(j):
        rr = pl.ds(j * KC, KC)
        return (pltpu.make_async_copy(outh.at[1, rr], h_out.at[rr], osem.at[0, j]),
                pltpu.make_async_copy(outg.at[1, rr], g_out.at[rr], osem.at[1, j]))

    def round_(t, carry):
        gather(t)
        for i in range(RB // RI):
            rr = pl.ds(i * RI, RI)
            hi, lo = split(wf[t, rr, :])
            whi[rr, :] = hi
            wlo[rr, :] = lo
        gw[...] = jnp.zeros_like(gw)
        lcopy(lc_in, t, (r, c0)).wait_recv()

        @pl.when(t == 0)
        def _():
            lcopy(lcb.at[0], 1, (r, c1)).start()
            cl[2].wait()

        @pl.when(t == 1)
        def _():
            cl[3].wait()

        def chunk(j, carry):
            rr = pl.ds(pl.multiple_of(j * KC, KC), KC)
            bulk(h_in, hb, hs, hr, t, j, (r, c0)).wait_recv()
            hh = split(hb[t, rr, :])
            lc = lcb[t, :, rr]
            gh[...] = jnp.zeros_like(gh)

            def inner(i, carry):
                ri = pl.ds(pl.multiple_of(i * RI, RI), RI)
                ww = (whi[ri, :], wlo[ri, :])
                pred = dot3(ww, hh, ((1,), (1,)))
                xc = cnt[t, ri, rr]
                xf = xc.astype(f32)
                diff = pred - (jnp.log(jnp.maximum(xf, 1.0)) + (log_total - lrt[ri, :] - lc))
                e = jnp.where(xc > 0, (0.1 + 0.25 * jnp.sqrt(xf)) * diff, jax.nn.sigmoid(diff)) * (1.0 / CB)
                ee = split(e)
                gwi = dot3(ee, hh, ((1,), (0,)))
                gw[pl.ds(i * (RI // SH // 2), RI // SH // 2)] += gwi.reshape(RI // SH // 2, 2, SH, D)
                gh[...] += dot3(ee, ww, ((0,), (0,)))
                return carry

            lax.fori_loop(0, RB // RI, inner, 0)
            bulk(g_in, gb, gs, gr, t, j, (r, c0)).wait_recv()
            g = gh[...]
            acc = gb[t, rr, :] + g * g
            outg[t, rr, :] = acc
            outh[t, rr, :] = hb[t, rr, :] - learn_rate * g / jnp.sqrt(acc)

            @pl.when(t == 0)
            def _():
                bulk(outh.at[0], hb, hs, hr, 1, j, (r, c1)).start()
                bulk(outg.at[0], gb, gs, gr, 1, j, (r, c1)).start()

            @pl.when(t == 1)
            def _():
                for q in out_copies(j):
                    q.start()

            return carry

        lax.fori_loop(0, K, chunk, 0)

        c1x = pltpu.make_async_remote_copy(gw.at[:, 1 - k], r1.at[t], s1s.at[t], s1r.at[t], device_id=cp, device_id_type=MESH)
        c1x.start()
        c1x.wait()
        s1[t] = gw[:, k] + r1[t]

        def xcopy(i, at):
            return [pltpu.make_async_remote_copy(s1.at[t, h * 4 + (x + 1 + i) % 4], r2.at[t, h, at], s2s.at[t, h, i], s2r.at[t, h, at],
                                                 device_id=xp[i], device_id_type=MESH) for h in range(2)]

        for i in range(3):
            for q in xcopy(i, x):
                q.start()
        for i in range(3):
            for q in xcopy(i, (x + 1 + i) % 4):
                q.wait_recv()
        for h in range(2):
            tot = s1[t, h * 4 + x]
            for i in range(3):
                tot = tot + r2[t, h, (x + 1 + i) % 4]
            s2[t, h] = tot
        zc = pltpu.make_async_remote_copy(s2.at[t, 1 - zh], r3.at[t], s3s.at[t], s3r.at[t], device_id=zp, device_id_type=MESH)
        zc.start()
        for i in range(3):
            for q in xcopy(i, x):
                q.wait_send()
        zc.wait()
        g = s2[t, zh] + r3[t]
        acc = wa[...] + g * g
        wa[...] = acc
        wn = wf[t, rows(r), :] - learn_rate * g / jnp.sqrt(acc)

        @pl.when(t == 0)
        def _():
            wf[1, rows(r), :] = wn
            own_sends(1)

        @pl.when(t == 1)
        def _():
            s2[0, 0] = wn
        return carry

    lax.fori_loop(0, 2, round_, 0)

    fin = [pltpu.make_async_copy(s2.at[0, 0], w_out, loc.at[0]), pltpu.make_async_copy(wa, wa_out, loc.at[1])]
    for q in fin:
        q.start()
    for t in range(2):
        lcopy(lc_in, t, (r, c0)).wait_send()
        for j in range(K):
            bulk(h_in, hb, hs, hr, t, j, (r, c0)).wait_send()
            bulk(g_in, gb, gs, gr, t, j, (r, c0)).wait_send()
    for j in range(K):
        for q in out_copies(j):
            q.wait()
    for q in fin:
        q.wait()


def fused(p0, p1, cid, w, wa, lr, h, g, lc, cnt):
    anyspace = pl.BlockSpec(memory_space=pl.ANY)
    vm = pl.BlockSpec(memory_space=pltpu.VMEM)
    dma = pltpu.SemaphoreType.DMA
    return pl.pallas_call(
        functools.partial(kernel, p0, p1),
        name=f"swivel_{p0}_{p1}",
        out_shape=[jax.ShapeDtypeStruct(a.shape, f32) for a in (w, wa, h, g)],
        in_specs=[anyspace, anyspace, vm, anyspace, anyspace, anyspace, anyspace],
        out_specs=[anyspace] * 4,
        scratch_shapes=[
            pltpu.VMEM((2, RB, D), f32),
            pltpu.VMEM((RB, D), bf16),
            pltpu.VMEM((RB, D), bf16),
            pltpu.VMEM((SH, D), f32),
            pltpu.VMEM((RB, 128), f32),
            pltpu.VMEM((2, CB, D), f32),
            pltpu.VMEM((2, CB, D), f32),
            pltpu.VMEM((2, 1, CB), f32),
            pltpu.VMEM((2, RB, CB), jnp.int32),
            pltpu.VMEM((N_ROW // 2, 2, SH, D), f32),
            pltpu.VMEM((KC, D), f32),
            pltpu.VMEM((2, 8, SH, D), f32),
            pltpu.VMEM((2, 8, SH, D), f32),
            pltpu.VMEM((2, 2, 4, SH, D), f32),
            pltpu.VMEM((2, 2, SH, D), f32),
            pltpu.VMEM((2, SH, D), f32),
            pltpu.VMEM((2, CB, D), f32),
            pltpu.VMEM((2, CB, D), f32),
            dma((2, K)), dma((2, K)), dma((2, K)), dma((2, K)),
            dma((2,)), dma((2,)),
            dma((2, 15)), dma((2, 16)),
            dma((2,)), dma((2,)),
            dma((2, 2, 3)), dma((2, 2, 4)),
            dma((2,)), dma((2,)),
            dma((4,)), dma((2, K)),
        ],
        compiler_params=pltpu.CompilerParams(collective_id=cid, has_side_effects=True, vmem_limit_bytes=40 << 20),
    )(w, wa, lr, h, g, lc, cnt)


def per_device(row_factors, row_accum, row_marginals, col_factors, col_accum, col_marginals, counts, plan):
    lr = jnp.log(row_marginals.astype(f32))
    lc = jnp.log(col_marginals[0].astype(f32))
    cnt = counts.reshape(2, RB, CB)
    top = N_COL - 1
    order = [(top, m) for m in range(1, top)] + [(m, top) for m in range(1, top)]
    which = jnp.where(plan[0] == top, plan[1] - 1, plan[0] + (top - 2))
    branches = [functools.partial(fused, p0, p1, i) for i, (p0, p1) in enumerate(order)]
    w, wa, h, g = lax.switch(which, branches, row_factors[0], row_accum[0], lr, col_factors[0, 0], col_accum[0, 0], lc, cnt)
    return w[None], wa[None], h[None, None], g[None, None]


def solution(mesh):
    in_specs = (
        P("col", "row", None),
        P("col", "row", None),
        P("col", None),
        P("row", "col", None, None),
        P("row", "col", None, None),
        P("row", "col", None),
        P(None, "col", None, "row", None),
        P(),
    )
    out_specs = (
        P("col", "row", None),
        P("col", "row", None),
        P("row", "col", None, None),
        P("row", "col", None, None),
    )
    return jax.shard_map(
        per_device, mesh=mesh, in_specs=in_specs, out_specs=out_specs, check_vma=False
    )
```

```python
import functools

import jax
import jax.numpy as jnp
from jax import lax
from jax.experimental import pallas as pl
from jax.experimental.pallas import tpu as pltpu
from jax.sharding import PartitionSpec as P

log_total = 11.5
learn_rate = 0.05
MESH = pl.DeviceIdType.MESH

N_ROW, N_COL = 16, 32
RB, CB, D = 512, 512, 256
SH = RB // N_ROW
K = 4
KC = CB // K
RI = 128
f32, bf16 = jnp.float32, jnp.bfloat16


def flip(v, mask):
    b = 0
    out = v
    while mask >> b:
        n = 0
        while mask >> (b + n) & 1:
            n += 1
        if n:
            field = lax.rem(lax.div(v, 1 << b), 1 << n)
            out = out + ((1 << n) - 1 - 2 * field) * (1 << b)
        b += n + 1
    return out


def split(a):
    hi = a.astype(bf16)
    return hi, (a - hi.astype(f32)).astype(bf16)


def dot3(a, b, dims):
    def d(p, q):
        return lax.dot_general(p, q, (dims, ((), ())), preferred_element_type=f32)

    return d(a[0], b[0]) + (d(a[0], b[1]) + d(a[1], b[0]))


def kernel(p0, p1, w_in, wa_in, lr_in, h_in, g_in, lc_in, cnt_in,
           w_out, wa_out, h_out, g_out,
           wf, whi, wlo, lrt, lcs, hb, gb, lcb, cnt, gw, gh, r1, s1, r2, s2, r3, outh, outg,
           bs, hr, gr, lrs, ags, agr, rss, rsr, loc):
    r = lax.axis_index("row")
    c = lax.axis_index("col")
    zh, k = lax.div(r, 8), lax.rem(r, 2)
    x = lax.rem(lax.div(r, 2), 4)
    other = 8 - 16 * zh
    zr = r + other
    zp = (zr, c)
    cp = (r + 1 - 2 * k, c)
    c0, c1 = (r, flip(c, p0)), (r, flip(c, p1))

    def xr(i):
        return zh * 8 + lax.rem(x + 1 + i, 4) * 2 + k

    def loop(n, body):
        def step(i, carry):
            body(i)
            return carry

        lax.fori_loop(0, n, step, 0)

    bar = pltpu.get_barrier_semaphore()
    for dev in (zp, cp, c0, c1):
        pl.semaphore_signal(bar, inc=1, device_id=dev, device_id_type=MESH)
    loop(3, lambda i: pl.semaphore_signal(bar, inc=1, device_id=(xr(i), c), device_id_type=MESH))

    def count_copy(t):
        return pltpu.make_async_copy(cnt_in.at[t, :, 0], cnt.at[t], loc.at[t])

    loop(2, lambda t: count_copy(t).start())
    lcs[...] = jnp.log(lc_in[...].astype(f32))

    def stand(i):
        ri = pl.ds(pl.multiple_of(i * 128, 128), 128)
        lr = jnp.log(lr_in[:, ri].astype(f32))
        lrt[ri, :] = jnp.transpose(jnp.broadcast_to(lr, (128, 128)))

    loop(4, stand)

    def rows(q):
        return pl.ds(q * SH, SH)

    wf[0, rows(r), :] = w_in[...]
    wa_out[...] = wa_in[...]
    pl.semaphore_wait(bar, 7)

    def send(src, dst, ss, rs, dev):
        return pltpu.make_async_remote_copy(src, dst, ss, rs, device_id=dev, device_id_type=MESH)

    def agcopy(t, q, slot, dev, src=None):
        ref = wf.at[t, rows(q)]
        return send(ref if src is None else src, ref, ags.at[t], agr.at[t, slot], dev)

    def to_peers(t, q, half, src=None):
        loop(3, lambda i: agcopy(t, q, 1 + half * 3 + i, (xr(2 - i), c), src).start())
        agcopy(t, q, 7, cp, src).start()

    def own_sends(t, src=None):
        agcopy(t, r, 0, zp, src).start()
        to_peers(t, r, 0, src)

    def gather(t):
        agcopy(t, zr, 0, zp).wait_recv()
        to_peers(t, zr, 1)

        def pass_on(i):
            q = xr(lax.rem(i, 3)) + lax.div(i, 3) * other
            agcopy(t, q, 1 + i, cp).wait_recv()
            agcopy(t, q, 7, cp).start()

        loop(6, pass_on)
        half = wf.at[t, pl.ds(0, RB // 2)]
        send(half, half, ags.at[t], agr.at[t, 7], cp).wait_recv()
        most = wf.at[t, pl.ds(0, RB - SH)]
        send(most, most, ags.at[t], agr.at[t, 7], cp).wait_send()

    def bulk(src, buf, n, rs, t, j, dev):
        rr = pl.ds(pl.multiple_of(j * KC, KC), KC)
        return send(src.at[rr], buf.at[t, rr], bs.at[t, n], rs.at[t, j], dev)

    def hcopy(t, j, src=h_in, dev=c0):
        return bulk(src, hb, 0, hr, t, j, dev)

    def gcopy(t, j, src=g_in, dev=c0):
        return bulk(src, gb, 1, gr, t, j, dev)

    def lcopy(src, t, dev):
        return send(src, lcb.at[t], bs.at[t, 2], lrs.at[t], dev)

    own_sends(0, w_in)
    lcopy(lcs, 0, c0).start()
    loop(K, lambda j: hcopy(0, j).start())
    loop(K, lambda j: gcopy(0, j).start())

    def round_(t):
        gather(t)

        def halves(i):
            ri = pl.ds(pl.multiple_of(i * 32, 32), 32)
            hi, lo = split(wf[t, ri, :])
            whi[ri, :] = hi
            wlo[ri, :] = lo
            gw[i] = jnp.zeros((SH, D), f32)
            gh[ri, :] = jnp.zeros((32, D), f32)

        loop(16, halves)
        count_copy(t).wait()
        lcopy(lcs, t, c0).wait_recv()

        @pl.when(t == 0)
        def _():
            lcopy(lcb.at[0], 1, c1).start()

        def chunk(j):
            rr = pl.ds(pl.multiple_of(j * KC, KC), KC)
            hcopy(t, j).wait_recv()
            hh = split(hb[t, rr, :])
            lc = lcb[t, :, rr]

            def inner(i):
                ri = pl.ds(pl.multiple_of(i * RI, RI), RI)
                ww = (whi[ri, :], wlo[ri, :])
                pred = dot3(ww, hh, ((1,), (1,)))
                xc = cnt[t, ri, rr]
                xf = xc.astype(f32)
                diff = pred - (jnp.log(jnp.maximum(xf, 1.0)) + (log_total - lrt[ri, :] - lc))
                e = jnp.where(xc > 0, (0.1 + 0.25 * jnp.sqrt(xf)) * diff, jax.nn.sigmoid(diff)) * (1.0 / CB)
                ee = split(e)
                gwi = dot3(ee, hh, ((1,), (0,)))
                gw[pl.ds(i * (RI // SH), RI // SH)] += gwi.reshape(RI // SH, SH, D)
                gh[rr, :] += dot3(ee, ww, ((0,), (0,)))

            loop(RB // RI, inner)

        loop(K, chunk)

        def core_shard(i):
            return send(gw.at[i * 2 + 1 - k], r1.at[t, i], rss.at[t, 0], rsr.at[t, 0], cp)

        def xcopy(i, h):
            q = lax.rem(x + 1 + i, 4)
            return send(s1.at[h * 4 + q], r2.at[t, h * 3 + 2 - i], rss.at[t, 1], rsr.at[t, 1], (xr(i), c))

        def zcopy():
            return send(s2.at[1 - zh], r3.at[t], rss.at[t, 2], rsr.at[t, 2], zp)

        loop(8, lambda i: core_shard(i).start())

        def update(j):
            gcopy(t, j).wait_recv()

            def part(n):
                ri = pl.ds(pl.multiple_of(j * KC + n * 32, 32), 32)
                g = gh[ri, :]
                acc = gb[t, ri, :] + g * g
                outg[t, ri, :] = acc
                outh[t, ri, :] = hb[t, ri, :] - learn_rate * g * lax.rsqrt(acc)

            loop(KC // 32, part)

            @pl.when(t == 0)
            def _():
                hcopy(1, j, outh.at[0], c1).start()

            @pl.when(j == 0)
            def _():
                send(r1.at[t], r1.at[t], rss.at[t, 0], rsr.at[t, 0], cp).wait()

                def add(i):
                    s1[i] = gw[i * 2 + k] + r1[t, i]

                loop(8, add)
                loop(6, lambda i: xcopy(lax.rem(i, 3), lax.div(i, 3)).start())

            @pl.when(j == 1)
            def _():
                send(r2.at[t], r2.at[t], rss.at[t, 1], rsr.at[t, 1], cp).wait()

                def total(h):
                    s2[h] = s1[h * 4 + x] + r2[t, h * 3] + (r2[t, h * 3 + 1] + r2[t, h * 3 + 2])

                loop(2, total)
                zcopy().start()

            @pl.when(j == 2)
            def _():
                zcopy().wait()
                sg = s2[zh] + r3[t]
                wacc = wa_out[...] + sg * sg
                wa_out[...] = wacc
                wn = wf[t, rows(r), :] - learn_rate * sg * lax.rsqrt(wacc)
                wf[1, rows(r), :] = wn
                w_out[...] = wn

                @pl.when(t == 0)
                def _():
                    own_sends(1)

        loop(K, update)

        @pl.when(t == 0)
        def _():
            loop(K, lambda j: gcopy(1, j, outg.at[0], c1).start())

        send(hb.at[t], hb.at[t], bs.at[t, 0], rsr.at[t, 0], c0).wait_send()

    loop(2, round_)
    ends = [pltpu.make_async_copy(outh.at[1], h_out, loc.at[0]), pltpu.make_async_copy(outg.at[1], g_out, loc.at[1])]
    for q in ends:
        q.start()

    def sent(t):
        send(gb.at[t], gb.at[t], bs.at[t, 1], rsr.at[t, 0], c0).wait_send()
        lcopy(lcs, t, c0).wait_send()

    loop(2, sent)
    for q in ends:
        q.wait()


def fused(p0, p1, cid, w, wa, lr, h, g, lc, cnt):
    anyspace = pl.BlockSpec(memory_space=pl.ANY)
    hbm = pl.BlockSpec(memory_space=pltpu.HBM)
    vm = pl.BlockSpec(memory_space=pltpu.VMEM)
    dma = pltpu.SemaphoreType.DMA
    return pl.pallas_call(
        functools.partial(kernel, p0, p1),
        name=f"swivel_{p0}_{p1}",
        out_shape=[jax.ShapeDtypeStruct(a.shape, f32) for a in (w, wa, h, g)],
        in_specs=[vm, vm, vm, hbm, hbm, vm, hbm],
        out_specs=[vm, vm, anyspace, anyspace],
        scratch_shapes=[
            pltpu.VMEM((2, RB, D), f32),
            pltpu.VMEM((RB, D), bf16),
            pltpu.VMEM((RB, D), bf16),
            pltpu.VMEM((RB, 128), f32),
            pltpu.VMEM((1, CB), f32),
            pltpu.VMEM((2, CB, D), f32),
            pltpu.VMEM((2, CB, D), f32),
            pltpu.VMEM((2, 1, CB), f32),
            pltpu.VMEM((2, RB, CB), jnp.int32),
            pltpu.VMEM((N_ROW, SH, D), f32),
            pltpu.VMEM((CB, D), f32),
            pltpu.VMEM((2, 8, SH, D), f32),
            pltpu.VMEM((8, SH, D), f32),
            pltpu.VMEM((2, 6, SH, D), f32),
            pltpu.VMEM((2, SH, D), f32),
            pltpu.VMEM((2, SH, D), f32),
            pltpu.VMEM((2, CB, D), f32),
            pltpu.VMEM((2, CB, D), f32),
            dma((2, 3)), dma((2, K)), dma((2, K)), dma((2,)),
            dma((2,)), dma((2, 8)), dma((2, 3)), dma((2, 3)), dma((2,)),
        ],
        compiler_params=pltpu.CompilerParams(collective_id=cid, has_side_effects=True, vmem_limit_bytes=56 << 20),
    )(w, wa, lr, h, g, lc, cnt)


def per_device(row_factors, row_accum, row_marginals, col_factors, col_accum, col_marginals, counts, plan):
    lr, lc = row_marginals, col_marginals[0]
    cnt = counts.reshape(2, RB, 1, CB)
    top = N_COL - 1
    order = [(top, m) for m in range(1, top)] + [(m, top) for m in range(1, top)]
    which = jnp.where(plan[0] == top, plan[1] - 1, plan[0] + (top - 2))
    branches = [functools.partial(fused, p0, p1, i) for i, (p0, p1) in enumerate(order)]
    w, wa, h, g = lax.switch(which, branches, row_factors[0], row_accum[0], lr, col_factors[0, 0], col_accum[0, 0], lc, cnt)
    return w[None], wa[None], h[None, None], g[None, None]


def solution(mesh):
    in_specs = (
        P("col", "row", None),
        P("col", "row", None),
        P("col", None),
        P("row", "col", None, None),
        P("row", "col", None, None),
        P("row", "col", None),
        P(None, "col", None, "row", None),
        P(),
    )
    out_specs = (
        P("col", "row", None),
        P("col", "row", None),
        P("row", "col", None, None),
        P("row", "col", None, None),
    )
    return jax.shard_map(
        per_device, mesh=mesh, in_specs=in_specs, out_specs=out_specs, check_vma=False
    )
```

```python
import functools

import jax
import jax.numpy as jnp
from jax import lax
from jax.experimental import pallas as pl
from jax.experimental.pallas import tpu as pltpu
from jax.sharding import PartitionSpec as P

log_total = 11.5
learn_rate = 0.05
MESH = pl.DeviceIdType.MESH

N_ROW, N_COL = 16, 32
RB, CB, D = 512, 512, 256
SH = RB // N_ROW
K = 4
KC = CB // K
RI = 128
f32, bf16 = jnp.float32, jnp.bfloat16


def flip(v, mask):
    b = 0
    out = v
    while mask >> b:
        n = 0
        while mask >> (b + n) & 1:
            n += 1
        if n:
            field = lax.rem(lax.div(v, 1 << b), 1 << n)
            out = out + ((1 << n) - 1 - 2 * field) * (1 << b)
        b += n + 1
    return out


def split(a):
    hi = a.astype(bf16)
    return hi, (a - hi.astype(f32)).astype(bf16)


def dot3(a, b, dims):
    (da,), (db,) = dims
    left = jnp.concatenate([a[0], a[0], a[1]], axis=da)
    right = jnp.concatenate([b[0], b[1], b[0]], axis=db)
    return lax.dot_general(left, right, (dims, ((), ())), preferred_element_type=f32)


def kernel(p0, p1, w_in, wa_in, lr_in, h_in, g_in, lc_in, cnt_in,
           w_out, wa_out, h_out, g_out,
           wf, whi, wlo, lrt, lcs, hb, gb, lcb, cnt, gw, gh, r1, s1, r2, s2, r3, outh, outg,
           bs, hr, gr, lrs, ags, agr, rss, rsr, loc):
    r = lax.axis_index("row")
    c = lax.axis_index("col")
    zh, k = lax.div(r, 8), lax.rem(r, 2)
    x = lax.rem(lax.div(r, 2), 4)
    other = 8 - 16 * zh
    zr = r + other
    zp = (zr, c)
    cp = (r + 1 - 2 * k, c)
    c0, c1 = (r, flip(c, p0)), (r, flip(c, p1))

    def xr(i):
        return zh * 8 + lax.rem(x + 1 + i, 4) * 2 + k

    def loop(n, body):
        def step(i, carry):
            body(i)
            return carry

        lax.fori_loop(0, n, step, 0)

    bar = pltpu.get_barrier_semaphore()
    for dev in (zp, cp, c0, c1):
        pl.semaphore_signal(bar, inc=1, device_id=dev, device_id_type=MESH)
    loop(3, lambda i: pl.semaphore_signal(bar, inc=1, device_id=(xr(i), c), device_id_type=MESH))

    def count_copy(t):
        return pltpu.make_async_copy(cnt_in.at[t, :, 0], cnt.at[t], loc.at[t])

    loop(2, lambda t: count_copy(t).start())
    lcs[...] = jnp.log(lc_in[...].astype(f32))

    def stand(i):
        ri = pl.ds(pl.multiple_of(i * 128, 128), 128)
        lr = jnp.log(lr_in[:, ri].astype(f32))
        lrt[ri, :] = jnp.transpose(jnp.broadcast_to(lr, (128, 128)))

    loop(4, stand)

    def rows(q):
        return pl.ds(q * SH, SH)

    wf[0, rows(r), :] = w_in[...]
    wa_out[...] = wa_in[...]
    pl.semaphore_wait(bar, 7)

    def send(src, dst, ss, rs, dev):
        return pltpu.make_async_remote_copy(src, dst, ss, rs, device_id=dev, device_id_type=MESH)

    def agcopy(t, q, slot, dev, src=None):
        ref = wf.at[t, rows(q)]
        return send(ref if src is None else src, ref, ags.at[t], agr.at[t, slot], dev)

    def to_peers(t, q, half, src=None):
        loop(3, lambda i: agcopy(t, q, 1 + half * 3 + i, (xr(2 - i), c), src).start())
        agcopy(t, q, 7, cp, src).start()

    def own_sends(t, src=None):
        agcopy(t, r, 0, zp, src).start()
        to_peers(t, r, 0, src)

    def gather(t):
        agcopy(t, zr, 0, zp).wait_recv()
        to_peers(t, zr, 1)

        def pass_on(i):
            q = xr(lax.rem(i, 3)) + lax.div(i, 3) * other
            agcopy(t, q, 1 + i, cp).wait_recv()
            agcopy(t, q, 7, cp).start()

        loop(6, pass_on)
        half = wf.at[t, pl.ds(0, RB // 2)]
        send(half, half, ags.at[t], agr.at[t, 7], cp).wait_recv()
        most = wf.at[t, pl.ds(0, RB - SH)]
        send(most, most, ags.at[t], agr.at[t, 7], cp).wait_send()

    def bulk(src, buf, n, rs, t, j, dev):
        rr = pl.ds(pl.multiple_of(j * KC, KC), KC)
        return send(src.at[rr], buf.at[t, rr], bs.at[t, n], rs.at[t, j], dev)

    def hcopy(t, j, src=h_in, dev=c0):
        return bulk(src, hb, 0, hr, t, j, dev)

    def gcopy(t, j, src=g_in, dev=c0):
        return bulk(src, gb, 1, gr, t, j, dev)

    def lcopy(src, t, dev):
        return send(src, lcb.at[t], bs.at[t, 2], lrs.at[t], dev)

    own_sends(0, w_in)
    lcopy(lcs, 0, c0).start()
    loop(K, lambda j: hcopy(0, j).start())
    loop(K, lambda j: gcopy(0, j).start())

    def round_(t):
        gather(t)

        def halves(i):
            ri = pl.ds(pl.multiple_of(i * 32, 32), 32)
            hi, lo = split(wf[t, ri, :])
            whi[ri, :] = hi
            wlo[ri, :] = lo
            gw[i] = jnp.zeros((SH, D), f32)
            gh[ri, :] = jnp.zeros((32, D), f32)

        loop(16, halves)
        count_copy(t).wait()
        lcopy(lcs, t, c0).wait_recv()

        @pl.when(t == 0)
        def _():
            lcopy(lcb.at[0], 1, c1).start()

        def chunk(j):
            rr = pl.ds(pl.multiple_of(j * KC, KC), KC)
            hcopy(t, j).wait_recv()
            hh = split(hb[t, rr, :])
            lc = lcb[t, :, rr]

            def inner(i):
                ri = pl.ds(pl.multiple_of(i * RI, RI), RI)
                ww = (whi[ri, :], wlo[ri, :])
                pred = dot3(ww, hh, ((1,), (1,)))
                xc = cnt[t, ri, rr]
                xf = xc.astype(f32)
                diff = pred - (jnp.log(jnp.maximum(xf, 1.0)) + (log_total - lrt[ri, :] - lc))
                e = jnp.where(xc > 0, (0.1 + 0.25 * jnp.sqrt(xf)) * diff, jax.nn.sigmoid(diff)) * (1.0 / CB)
                ee = split(e)
                gwi = dot3(ee, hh, ((1,), (0,)))
                gw[pl.ds(i * (RI // SH), RI // SH)] += gwi.reshape(RI // SH, SH, D)
                gh[rr, :] += dot3(ee, ww, ((0,), (0,)))

            loop(RB // RI, inner)

        loop(K, chunk)

        def core_shard(i):
            return send(gw.at[i * 2 + 1 - k], r1.at[t, i], rss.at[t, 0], rsr.at[t, 0], cp)

        def xcopy(i, h):
            q = lax.rem(x + 1 + i, 4)
            return send(s1.at[h * 4 + q], r2.at[t, h * 3 + 2 - i], rss.at[t, 1], rsr.at[t, 1], (xr(i), c))

        def zcopy():
            return send(s2.at[1 - zh], r3.at[t], rss.at[t, 2], rsr.at[t, 2], zp)

        loop(8, lambda i: core_shard(i).start())

        def update(j):
            gcopy(t, j).wait_recv()

            def part(n):
                ri = pl.ds(pl.multiple_of(j * KC + n * 32, 32), 32)
                g = gh[ri, :]
                acc = gb[t, ri, :] + g * g
                outg[t, ri, :] = acc
                outh[t, ri, :] = hb[t, ri, :] - learn_rate * g * lax.rsqrt(acc)

            loop(KC // 32, part)

            @pl.when(t == 0)
            def _():
                hcopy(1, j, outh.at[0], c1).start()

            @pl.when(j == 0)
            def _():
                send(r1.at[t], r1.at[t], rss.at[t, 0], rsr.at[t, 0], cp).wait()

                def add(i):
                    s1[i] = gw[i * 2 + k] + r1[t, i]

                loop(8, add)
                loop(6, lambda i: xcopy(lax.rem(i, 3), lax.div(i, 3)).start())

            @pl.when(j == 1)
            def _():
                send(r2.at[t], r2.at[t], rss.at[t, 1], rsr.at[t, 1], cp).wait()

                def total(h):
                    s2[h] = s1[h * 4 + x] + r2[t, h * 3] + (r2[t, h * 3 + 1] + r2[t, h * 3 + 2])

                loop(2, total)
                zcopy().start()

            @pl.when(j == 2)
            def _():
                zcopy().wait()
                sg = s2[zh] + r3[t]
                wacc = wa_out[...] + sg * sg
                wa_out[...] = wacc
                wn = wf[t, rows(r), :] - learn_rate * sg * lax.rsqrt(wacc)
                wf[1, rows(r), :] = wn
                w_out[...] = wn

                @pl.when(t == 0)
                def _():
                    own_sends(1)

        loop(K, update)

        @pl.when(t == 0)
        def _():
            loop(K, lambda j: gcopy(1, j, outg.at[0], c1).start())

        send(hb.at[t], hb.at[t], bs.at[t, 0], rsr.at[t, 0], c0).wait_send()

    loop(2, round_)
    ends = [pltpu.make_async_copy(outh.at[1], h_out, loc.at[0]), pltpu.make_async_copy(outg.at[1], g_out, loc.at[1])]
    for q in ends:
        q.start()

    def sent(t):
        send(gb.at[t], gb.at[t], bs.at[t, 1], rsr.at[t, 0], c0).wait_send()
        lcopy(lcs, t, c0).wait_send()

    loop(2, sent)
    for q in ends:
        q.wait()


def fused(p0, p1, cid, w, wa, lr, h, g, lc, cnt):
    anyspace = pl.BlockSpec(memory_space=pl.ANY)
    hbm = pl.BlockSpec(memory_space=pltpu.HBM)
    vm = pl.BlockSpec(memory_space=pltpu.VMEM)
    dma = pltpu.SemaphoreType.DMA
    return pl.pallas_call(
        functools.partial(kernel, p0, p1),
        name=f"swivel_{p0}_{p1}",
        out_shape=[jax.ShapeDtypeStruct(a.shape, f32) for a in (w, wa, h, g)],
        in_specs=[vm, vm, vm, hbm, hbm, vm, hbm],
        out_specs=[vm, vm, anyspace, anyspace],
        scratch_shapes=[
            pltpu.VMEM((2, RB, D), f32),
            pltpu.VMEM((RB, D), bf16),
            pltpu.VMEM((RB, D), bf16),
            pltpu.VMEM((RB, 128), f32),
            pltpu.VMEM((1, CB), f32),
            pltpu.VMEM((2, CB, D), f32),
            pltpu.VMEM((2, CB, D), f32),
            pltpu.VMEM((2, 1, CB), f32),
            pltpu.VMEM((2, RB, CB), jnp.int32),
            pltpu.VMEM((N_ROW, SH, D), f32),
            pltpu.VMEM((CB, D), f32),
            pltpu.VMEM((2, 8, SH, D), f32),
            pltpu.VMEM((8, SH, D), f32),
            pltpu.VMEM((2, 6, SH, D), f32),
            pltpu.VMEM((2, SH, D), f32),
            pltpu.VMEM((2, SH, D), f32),
            pltpu.VMEM((2, CB, D), f32),
            pltpu.VMEM((2, CB, D), f32),
            dma((2, 3)), dma((2, K)), dma((2, K)), dma((2,)),
            dma((2,)), dma((2, 8)), dma((2, 3)), dma((2, 3)), dma((2,)),
        ],
        compiler_params=pltpu.CompilerParams(collective_id=cid, has_side_effects=True, vmem_limit_bytes=56 << 20),
    )(w, wa, lr, h, g, lc, cnt)


def per_device(row_factors, row_accum, row_marginals, col_factors, col_accum, col_marginals, counts, plan):
    lr, lc = row_marginals, col_marginals[0]
    cnt = counts.reshape(2, RB, 1, CB)
    top = N_COL - 1
    order = [(top, m) for m in range(1, top)] + [(m, top) for m in range(1, top)]
    which = jnp.where(plan[0] == top, plan[1] - 1, plan[0] + (top - 2))
    branches = [functools.partial(fused, p0, p1, i) for i, (p0, p1) in enumerate(order)]
    w, wa, h, g = lax.switch(which, branches, row_factors[0], row_accum[0], lr, col_factors[0, 0], col_accum[0, 0], lc, cnt)
    return w[None], wa[None], h[None, None], g[None, None]


def solution(mesh):
    in_specs = (
        P("col", "row", None),
        P("col", "row", None),
        P("col", None),
        P("row", "col", None, None),
        P("row", "col", None, None),
        P("row", "col", None),
        P(None, "col", None, "row", None),
        P(),
    )
    out_specs = (
        P("col", "row", None),
        P("col", "row", None),
        P("row", "col", None, None),
        P("row", "col", None, None),
    )
    return jax.shard_map(
        per_device, mesh=mesh, in_specs=in_specs, out_specs=out_specs, check_vma=False
    )
```
